32 devices in a mesh: rows: 8 (over z, y), cols: 4 (over x, core).
Axes of the slice: x: 2, y: 2, z: 4, core: 2. Of those that a mesh axis runs over, the one named last changes fastest.
Arguments:
- coefficients: float32 [4, 1024, 4, 256], P(None, 'rows'), may hold values from -0.03 to 0.09
- support: int32 [4, 1024, 4], P(None, 'rows'), may hold values from 0 to 11, all different within a row
- primal: float32 [12, 256, 256], P('cols'), may hold values from -0.5 to 9, as said below
- dual_inverse: float32 [12, 256, 256], P('cols'), may hold values from -0.5 to 9, as said below
- block_sizes: int32 [12], P('cols'), may hold values from 64 to 256, as said below
- damping: float32 [4, 1024], P(None, 'rows'), may hold values from 0.5 to 2
- right_sides: float32 [4, 32, 1024], P(None, 'cols', 'rows'), may hold values from -6 to 6
Outputs:
- updated: float32 [4, 1024, 4096], P(None, 'rows', 'cols')
- panel_factor: float32 [4, 1024, 128], P(None, 'rows')
- solved: float32 [4, 32, 1024], P(None, 'cols', 'rows')
The draws below stay inside these ranges and needn't reach their ends.
Inputs may be any that keep to these rules, and one draw needn't show every extreme that they name: `primal`: each block is symmetric positive definite. `dual_inverse`: each block is symmetric positive definite. `block_sizes`: some block has order 256.
All inputs are finite; a program needn't handle non-finite values.
Results may differ from the reference program's by a relative error of at most 0.00015.
Values sent between devices are 32-bit elements; how exact they have to be, the bound alone decides.
A program may use at most 192 MiB of HBM per device.

```python
import math
import jax
import jax.numpy as jnp
from jax import lax

BS = 256
K = 4
TILE = 128
NRHS = 32
TPR = 4
SPAN = 1024
NB = 12
N_ROWS = 8


def definite_blocks(key):
    first_key, second_key = jax.random.split(key)
    floor_value, ceiling, spread = (1.0, 4.0, 0.4)
    diagonal = jnp.exp(jax.random.uniform(first_key, (NB, BS), jnp.float32, math.log(floor_value), math.log(ceiling)))
    noise = jax.random.normal(second_key, (NB, BS, BS), jnp.float32) * (spread / math.sqrt(BS))
    symmetric = (noise + jnp.swapaxes(noise, 1, 2)) / math.sqrt(2.0)
    return symmetric + diagonal[:, :, None] * jnp.eye(BS, dtype=jnp.float32)[None, :, :]


def draw_primal(key, part):
    return definite_blocks(jax.random.fold_in(key, 11))


def draw_dual_inverse(key, part):
    return definite_blocks(jax.random.fold_in(key, 23))


def draw_block_sizes(key, part):
    orders = jax.random.randint(jax.random.fold_in(key, 31), (NB,), BS // 4, BS + 1)
    picked = jax.random.randint(jax.random.fold_in(key, 37), (), 0, NB)
    return jnp.where(jnp.arange(NB) == picked, BS, orders).astype(jnp.int32)


def block_levels(rng, extent, pieces, least, high):
    loudness, own = 1.0, jax.random.fold_in(rng, 6)
    for position, blocks in pieces:
        draws = jnp.exp(jax.random.uniform(jax.random.fold_in(own, position), (blocks,), jnp.float32, least / len(pieces), high / len(pieces)))
        loudness = loudness * jnp.repeat(draws, extent[position] // blocks).reshape([-1 if axis == position else 1 for axis in range(len(extent))])
    return loudness


def different_ones(stream_key, rows, number_of, top, lift):
    sequence = jax.random.permutation(jax.random.fold_in(stream_key, 1), number_of)
    pull = sequence
    for power in range(3):
        pull = pull * pull // number_of
    pull = pull * lift // number_of
    chance = jax.random.randint(jax.random.fold_in(stream_key, 2), (rows, number_of), 0, 4096) + pull
    fixed_rows = jax.random.permutation(jax.random.fold_in(stream_key, 3), rows)[jnp.arange(number_of) % rows]
    chance = jnp.where(jnp.arange(rows)[:, None] == fixed_rows[None, :], 1 << 14, chance)
    merit = chance * number_of + jnp.arange(number_of)
    return lax.top_k(merit.astype(jnp.int32), top)[1].astype(jnp.int32)


def gaussian(stream_key, extent, scale, reach, pieces=(), kind=jnp.bfloat16):
    drawn = jax.random.normal(stream_key, extent, jnp.float32) * scale
    if len(pieces) > 0:
        drawn = block_levels(stream_key, extent, pieces, -0.22, 0.18) * drawn
    return jnp.clip(drawn, min=-reach, max=reach).astype(kind)


def setup_inputs(seed: int = 0) -> dict:
    streams_of = jax.random.split(jax.random.key(seed), 8)
    return {
        "coefficients": jnp.clip(-0.03 + 0.120000003 * jax.random.uniform(streams_of[0], (TPR, SPAN, K, BS), jnp.float32) ** block_levels(streams_of[0], (TPR, SPAN, K, BS), ((1, 8),), -0.2, 0.2), -0.03, 0.09),
        "support": different_ones(streams_of[1], TPR * SPAN, NB, K, 5461).reshape((TPR, SPAN, K)),
        "primal": draw_primal(jax.random.fold_in(streams_of[7], 71), 0),
        "dual_inverse": draw_dual_inverse(jax.random.fold_in(streams_of[7], 71), 0),
        "block_sizes": draw_block_sizes(jax.random.fold_in(streams_of[7], 71), 0),
        "damping": jnp.clip(jnp.exp(math.log(2.0) - 1.3862944 * jax.random.uniform(streams_of[5], (TPR, SPAN), jnp.float32) ** block_levels(streams_of[5], (TPR, SPAN), ((1, 8),), -0.2, 0.2)), 0.5, 2.0),
        "right_sides": gaussian(streams_of[6], (TPR, NRHS, SPAN), 1.0, 6.0, ((1, 4), (2, 8)), jnp.float32),
    }


highest = lax.Precision.HIGHEST

def reference(coefficients, support, primal, dual_inverse, block_sizes, damping, right_sides):
    count_all = TPR * TILE * N_ROWS
    flat_coef = coefficients.reshape(count_all, K, BS)
    flat_support = support.reshape(count_all, K)
    positions = jnp.arange(BS, dtype=jnp.int32)
    schur_full = jnp.zeros((count_all, count_all), jnp.float32)
    for block_id in range(NB):
        chosen = (flat_support == block_id).astype(jnp.float32)
        dense_rows = jnp.einsum('mk,mkd->md', chosen, flat_coef, precision=highest)
        active = (positions < block_sizes[block_id]).astype(jnp.float32)
        weights = primal[block_id] * dual_inverse[block_id] * active[:, None] * active[None, :]
        weighted = jnp.dot(dense_rows.astype(jnp.float32), weights.astype(jnp.float32), precision=highest, preferred_element_type=jnp.float32)
        schur_full = schur_full + jnp.dot(weighted.astype(jnp.float32), dense_rows.T.astype(jnp.float32), precision=highest, preferred_element_type=jnp.float32)
    schur_full = schur_full + jnp.diag(damping.reshape(count_all))
    corner = schur_full[:TILE, :TILE]
    factor = jnp.linalg.cholesky(corner)
    identity = jnp.eye(TILE, dtype=jnp.float32)
    inverse = jax.scipy.linalg.solve_triangular(factor, identity, lower=True)
    panel_rows = jnp.dot(schur_full[:, :TILE].astype(jnp.float32), inverse.T.astype(jnp.float32), precision=highest, preferred_element_type=jnp.float32)
    outer_term = jnp.dot(panel_rows.astype(jnp.float32), panel_rows.T.astype(jnp.float32), precision=highest, preferred_element_type=jnp.float32)
    later = jnp.arange(count_all) >= TILE
    updated = schur_full - jnp.where(later[:, None] & later[None, :], outer_term, 0.0)
    all_sides = jnp.transpose(right_sides, (1, 0, 2)).reshape(NRHS, count_all)
    leading = jnp.dot(all_sides[:, :TILE].astype(jnp.float32), inverse.T.astype(jnp.float32), precision=highest, preferred_element_type=jnp.float32)
    remainder = all_sides - jnp.dot(leading.astype(jnp.float32), panel_rows.T.astype(jnp.float32), precision=highest, preferred_element_type=jnp.float32)
    padded_lead = jnp.pad(leading, ((0, 0), (0, count_all - TILE)))
    solved = jnp.where(later[None, :], remainder, padded_lead)
    solved = jnp.transpose(solved.reshape(NRHS, TPR, N_ROWS * TILE), (1, 0, 2))
    return (updated.reshape(TPR, N_ROWS * TILE, count_all), panel_rows.reshape(TPR, N_ROWS * TILE, TILE), solved)
```

```python
import functools

import jax
import jax.numpy as jnp
from jax import lax
from jax.experimental import pallas as pl
from jax.experimental.pallas import tpu as pltpu
from jax.sharding import PartitionSpec as P

TILE = 128

MESH = pl.DeviceIdType.MESH
highest = lax.Precision.HIGHEST
f32, bf16 = jnp.float32, jnp.bfloat16


def split(x):
    top = x.astype(bf16)
    return top, (x - top.astype(f32)).astype(bf16)


def product(a, b, dims, precision=None):
    return lax.dot_general(a, b, (dims, ((), ())), precision=precision, preferred_element_type=f32)


def exchange(rows, cols, coef_ref, primal_ref, dual_ref, sizes_ref, names_ref, damp_ref, sides_ref,
             updated_out, panel_out, solved_out,
             tiles, names_all, own, leads, lead_names, lead_damp, lead_sides, primal, dual, w_all,
             own_hi, own_lo, label_own, col_hi, col_lo, label_col, d_top, d_low, c_top, c_low,
             g_top, g_low, acc, schur, lead_schur, work, q_cat,
             local_sem, out_sem, fwd_s, fwd_r, bwd_s, bwd_r, fname_s, fname_r, bname_s, bname_r,
             lead_s, lead_r, share_s, share_r, pass_s, pass_r, wx_s, wx_r, wp_s, wp_r):
    r = lax.axis_index("rows")
    c = lax.axis_index("cols")
    half = rows // 2
    last = half - 1
    odd = r % 2
    pos = (1 - odd) * (r // 2) + odd * (rows - 1 - r // 2)

    def row_at(p):
        p = (p + rows) % rows
        upper = p // half
        return (1 - upper) * (2 * p) + upper * (2 * (rows - 1 - p) + 1)

    right = row_at(pos + 1)
    left = row_at(pos - 1)
    partner = c + 1 - 2 * (c % 2)
    near = jnp.minimum(pos, rows - pos)
    far = range(1, cols // 2)

    layers, lines, _ = coef_ref.shape
    slots = names_ref.shape[1]
    own_blocks, order, _ = primal_ref.shape
    blocks = cols * own_blocks
    height = layers * TILE
    full = layers
    groups = order // TILE
    layer = (c * (height * rows // cols)) // (rows * TILE)
    chunk = lines // cols

    def send(src, dst, s, v, row=None, col=None):
        return pltpu.make_async_remote_copy(
            src_ref=src, dst_ref=dst, send_sem=s, recv_sem=v,
            device_id=(r if row is None else row, c if col is None else col), device_id_type=MESH)

    loads = [pltpu.make_async_copy(primal_ref, primal, local_sem.at[0]),
             pltpu.make_async_copy(dual_ref, dual, local_sem.at[1]),
             pltpu.make_async_copy(coef_ref, own, local_sem.at[2])]
    for copy in loads:
        copy.start()

    barrier = pltpu.get_barrier_semaphore()
    for row in (right, left):
        pl.semaphore_signal(barrier, inc=1, device_id=(row, c), device_id_type=MESH)
    pl.semaphore_signal(barrier, inc=1, device_id=(r, partner), device_id_type=MESH)
    for k in far:
        pl.semaphore_signal(barrier, inc=1, device_id=(r, (c + 2 * k) % cols), device_id_type=MESH)

    loads[0].wait()
    loads[1].wait()
    across = lax.broadcasted_iota(jnp.int32, (order, order), 1)
    along = lax.broadcasted_iota(jnp.int32, (order, order), 0)
    for i in range(own_blocks):
        size = sizes_ref[i]
        w_all[c * own_blocks + i] = jnp.where((along < size) & (across < size), primal[i] * dual[i], 0.0)
    pl.semaphore_wait(barrier, 3 + len(far))

    waits = []

    def part(h):
        return pl.ds(h * (lines // 2), lines // 2)

    def fwd(s, h):
        row = row_at(pos - s)
        src = coef_ref.at[layer, part(h)] if s == 0 else tiles.at[row, part(h)]
        return send(src, tiles.at[row, part(h)], fwd_s.at[s, h], fwd_r.at[s, h], row=right)

    def bwd(s, h):
        row = row_at(pos + s)
        src = coef_ref.at[layer, part(h)] if s == 0 else tiles.at[row, part(h)]
        return send(src, tiles.at[row, part(h)], bwd_s.at[s, h], bwd_r.at[s, h], row=left)

    def fwd_name(s):
        row = row_at(pos - s)
        src = names_ref.at[layer] if s == 0 else names_all.at[row]
        return send(src, names_all.at[row], fname_s.at[s], fname_r.at[s], row=right)

    def bwd_name(s):
        row = row_at(pos + s)
        src = names_ref.at[layer] if s == 0 else names_all.at[row]
        return send(src, names_all.at[row], bname_s.at[s], bname_r.at[s], row=left)

    mine = pl.ds(pl.multiple_of(c * chunk, chunk), chunk)
    lead_own = [(coef_ref.at[0, mine], leads.at[mine]), (names_ref.at[0], lead_names),
                (damp_ref, lead_damp), (sides_ref.at[0], lead_sides)]
    lead_all = [(leads.at[mine], leads.at[mine]), (lead_names, lead_names),
                (lead_damp, lead_damp), (lead_sides, lead_sides)]

    def lead_to(pieces, way, row):
        return [send(src, dst, lead_s.at[way, m], lead_r.at[m], row=row) for m, (src, dst) in enumerate(pieces)]

    lead_local = [pltpu.make_async_copy(src, dst, local_sem.at[3 + m]) for m, (src, dst) in enumerate(lead_own)]

    @pl.when(r == 0)
    def _():
        for copy in lead_to(lead_own, 0, right) + lead_to(lead_own, 1, left) + lead_local:
            copy.start()

    def first(h):
        fwd(0, h).start()
        bwd(0, h).start()

    def wx(k, i, source=None):
        b = (c if source is None else source) * own_blocks + i
        return send(w_all.at[b], w_all.at[b], wx_s.at[k, i], wx_r.at[k, i], col=(c + 2 * k) % cols)

    def wp(k, i, source):
        b = source * own_blocks + i
        return send(w_all.at[b], w_all.at[b], wp_s.at[k, i], wp_r.at[k, i], col=partner)

    first(0)
    fwd_name(0).start()
    bwd_name(0).start()
    for i in range(own_blocks):
        for k in far:
            wx(k, i).start()
            waits.append(wx(k, i))
        wp(0, i, c).start()
        waits.append(wp(0, i, c))

    @pl.when(near >= 2)
    def _():
        first(1)

    def unpack(raw, hi, lo, at):
        for k in range(slots):
            for h in range(groups):
                top, low = split(raw[pl.ds(h * slots + k, TILE, stride=slots * groups), :])
                hi[k, at, h * TILE:(h + 1) * TILE] = top
                lo[k, at, h * TILE:(h + 1) * TILE] = low

    def put_labels(dst, at, names):
        names = names.astype(f32)
        turned = jnp.transpose(jnp.concatenate([names] * (8 // slots), axis=0))
        for k in range(slots):
            dst[k, at, :] = jnp.broadcast_to(turned[:, k:k + 1], (TILE, TILE)).astype(bf16)

    def called(b):
        return jnp.full((TILE, TILE), b.astype(f32)).astype(bf16)

    def pick(source, name):
        hi, lo, label, at = source
        top = low = jnp.zeros((TILE, order), bf16)
        for k in range(slots):
            hit = label[k, at, :] == name
            hit = jnp.concatenate([hit] * groups, axis=1)
            top = jnp.where(hit, hi[k, at, :], top)
            low = jnp.where(hit, lo[k, at, :], low)
        return top, low

    def own_tile(t):
        at = t * TILE
        return own_hi, own_lo, label_own, pl.ds(at if isinstance(t, int) else pl.multiple_of(at, TILE), TILE)

    def weigh(b, begin, stop):
        name = called(b)
        for t in range(begin, stop):
            top, low = pick(own_tile(t), name)
            at = pl.ds(t * TILE, TILE)
            d_top[at, :] = top
            d_low[at, :] = low
        span = pl.ds(begin * TILE, (stop - begin) * TILE)
        w_top, w_low = split(w_all[b])
        top, low = split(product(
            jnp.concatenate([d_top[span, :], d_top[span, :], d_low[span, :]], axis=1),
            jnp.concatenate([w_top, w_low, w_top], axis=0), ((1,), (0,))))
        g_top[b, span, :] = top
        g_low[b, span, :] = low

    loads[2].wait()
    for t in range(full):
        put_labels(label_own, pl.ds(t * TILE, TILE), names_ref[t])
        unpack(own.at[t], own_hi, own_lo, pl.ds(t * TILE, TILE))

    def weigh_source(source):
        def body(i, carry):
            weigh(source * own_blocks + i, 0, full)
            return carry
        lax.fori_loop(0, own_blocks, body, 0)

    weigh_source(c)

    def lead_step():
        @pl.when(r != 0)
        def _():
            for copy in lead_to(lead_all, 0, right):
                copy.wait_recv()

        @pl.when((pos >= 1) & (pos < half))
        def _():
            for copy in lead_to(lead_all, 0, right):
                copy.start()

        @pl.when(pos >= half + 2)
        def _():
            for copy in lead_to(lead_all, 1, left):
                copy.start()

        @pl.when(r == 0)
        def _():
            for copy in lead_local:
                copy.wait()

        for k in far:
            share(k).start()
        hand(0, c).start()

    def share(k):
        return send(leads.at[mine], leads.at[mine], share_s.at[k], share_r.at[k], col=(c + 2 * k) % cols)

    def piece(source):
        return pl.ds(pl.multiple_of(source * chunk, chunk), chunk)

    def hand(k, source):
        return send(leads.at[piece(source)], leads.at[piece(source)], pass_s.at[k], pass_r.at[k], col=partner)

    def ring(s, h):
        fwd(s - 1, h).wait_recv()
        if s < last or h == 0:
            fwd(s, h).start()
        bwd(s - 1, h).wait_recv()
        if s < last or h == 1:
            bwd(s, h).start()
        if h == 0:
            fwd_name(s - 1).wait_recv()
            bwd_name(s - 1).wait_recv()
            fwd_name(s).start()
            if s < last:
                bwd_name(s).start()

    def forward(i):
        for k in far:
            source = (c + cols - 2 * k) % cols
            wx(k, i).wait_recv()
            wp(k, i, source).start()
            waits.append(wp(k, i, source))

    def weigh_far(i):
        def body(j, carry):
            k = 1 + j // 2
            side = j % 2
            source = ((1 - side) * c + side * partner + cols - 2 * k) % cols
            weigh(source * own_blocks + i, 0, full)
            return carry
        for k in far:
            wp(k, i, c).wait_recv()
        lax.fori_loop(0, 2 * len(far), body, 0)

    pl.when(near < 3)(lead_step)

    @pl.when(near < 2)
    def _():
        first(1)

    for i in range(own_blocks):
        wp(0, i, c).wait_recv()
    weigh_source(partner)
    pending = [(s, h) for s in range(1, half) for h in range(2)]

    def serve(count):
        for _ in range(count):
            if pending:
                ring(*pending.pop(0))

    serve(1)
    forward(0)
    if own_blocks > 1:
        forward(1)
    pl.when(near == 3)(lead_step)
    serve(1)
    for i in range(2, own_blocks):
        forward(i)
    for i in range(min(2, own_blocks)):
        weigh_far(i)
    serve(1)
    pl.when(near > 3)(lead_step)
    for i in range(2, own_blocks):
        weigh_far(i)
    for k in far:
        share(k).wait_recv()
        hand(k, (c + cols - 2 * k) % cols).start()
    hand(0, c).wait_recv()
    for k in far:
        hand(k, c).wait_recv()

    put_labels(label_own, pl.ds(height, TILE), lead_names[...])
    unpack(leads, own_hi, own_lo, pl.ds(height, TILE))

    def weigh_lead(b, carry):
        weigh(b, full, full + 1)
        return carry

    lax.fori_loop(0, blocks, weigh_lead, 0)

    lane = lax.broadcasted_iota(jnp.int32, (TILE, TILE), 1)
    line = lax.broadcasted_iota(jnp.int32, (TILE, TILE), 0)
    fold = max(u for u in range(1, 5) if blocks % u == 0)
    rounds = blocks // fold
    low_rows = pl.ds(height, TILE)

    def double(sources, begin, size):
        acc[:2 * size, :] = jnp.zeros((2 * size, 2 * TILE), f32)

        def body(n, carry):
            for u in range(fold):
                top, low = pick(sources, called(n * fold + u))
                c_top[u, :TILE, :] = top
                c_top[u, TILE:, :] = low
            span = pl.ds(begin, size)
            a_top = jnp.concatenate([g_top[n * fold + u, span, :] for u in range(fold)], axis=1)
            a_low = jnp.concatenate([g_low[n * fold + u, span, :] for u in range(fold)], axis=1)
            both = jnp.concatenate([c_top[u] for u in range(fold)], axis=1)
            acc[:2 * size, :] += product(jnp.concatenate([a_top, a_low], axis=0), both, ((1,), (1,)))
            return carry

        lax.fori_loop(0, rounds, body, 0)
        return (acc[:size, :TILE] + (acc[:size, TILE:] + acc[size:2 * size, :TILE])) + acc[size:2 * size, TILE:]

    def eye(values):
        return jnp.where(lane == line, jnp.broadcast_to(values, (TILE, TILE)), 0.0)

    work[:, :TILE] = double(own_tile(full), height, TILE) + eye(lead_damp[0:1, :])
    work[:, TILE:] = jnp.where(lane == line, 1.0, 0.0)

    def eliminate(j):
        at = jnp.minimum(j, TILE - 1)
        pivot = work[pl.ds(at, 1), :]
        column = jnp.sum(jnp.where(lane == at, work[:, :TILE], 0.0), axis=1, keepdims=True)
        scale = jnp.sum(jnp.where(lane[0:1] == at, pivot[:, :TILE], 0.0), axis=1, keepdims=True)
        factor = jnp.where(line[:, 0:1] > j, column, 0.0) / scale
        work[...] = work[...] - factor * pivot

    steps = -(-TILE // (half * rounds))
    tall = height + TILE

    def group(sources, outs, begin):
        acc[:tall, :] = jnp.zeros((tall, 2 * TILE), f32)

        def body(n, carry):
            for u in range(fold):
                name = called(n * fold + u)
                for i, source in enumerate(sources):
                    at = pl.ds(i * TILE, TILE)
                    top, low = pick(source, name)
                    c_top[u, at, :] = top
                    c_low[u, at, :] = low
            a_top = [g_top[n * fold + u] for u in range(fold)]
            a_low = [g_low[n * fold + u] for u in range(fold)]
            b_top = [c_top[u] for u in range(fold)]
            b_low = [c_low[u] for u in range(fold)]
            acc[:tall, :] += product(
                jnp.concatenate(a_top + a_top + a_low, axis=1), jnp.concatenate(b_top + b_low + b_top, axis=1), ((1,), (1,)))
            for e in range(steps):
                eliminate(begin + n * steps + e)
            return carry

        lax.fori_loop(0, rounds, body, 0)
        for i, out in enumerate(outs):
            if out is None:
                lead_schur[...] = acc[:tall, i * TILE:(i + 1) * TILE]
            else:
                schur[:, columns(out)] = acc[:tall, i * TILE:(i + 1) * TILE]

    def columns(row):
        return pl.ds(pl.multiple_of(row * TILE, TILE), TILE)

    def remote(row, i):
        at = pl.ds(i * TILE, TILE)
        unpack(tiles.at[row], col_hi, col_lo, at)
        put_labels(label_col, at, names_all[row])
        return col_hi, col_lo, label_col, at

    group([own_tile(full), own_tile(layer)], [None, r], 0)
    here = pl.ds(pl.multiple_of(layer * TILE, TILE), TILE)
    schur[here, columns(r)] = schur[here, columns(r)] + eye(damp_ref[pl.ds(layer, 1), :])
    serve(1)
    for g in range(1, half):
        while pending and pending[0][0] <= g:
            serve(1)
        ahead, behind = row_at(pos - g), row_at(pos + g)
        group([remote(ahead, 0), remote(behind, 1)], [ahead, behind], g * rounds * steps)
        serve(1)

    diagonal = jnp.sum(jnp.where(lane == line, work[:, :TILE], 0.0), axis=1, keepdims=True)
    inverse = work[:, TILE:] / jnp.sqrt(diagonal)
    top_row = (r == 0).astype(f32)
    lead_schur[:TILE, :] = lead_schur[:TILE, :] + eye(damp_ref[0:1, :]) * top_row
    panel = product(lead_schur[:height, :], inverse, ((1,), (1,)), highest)
    panel_out[...] = panel
    q = product(panel, inverse, ((1,), (0,)), highest)
    q = jnp.concatenate([q[:TILE] * (1.0 - top_row), q[TILE:]], axis=0)
    q_top, q_low = split(q)
    q_cat[...] = jnp.concatenate([q_top, q_top, q_low], axis=1)
    leading = product(lead_sides[...], inverse, ((1,), (1,)), highest)
    remainder = product(leading, panel, ((1,), (1,)), highest)
    for t in range(layers):
        value = sides_ref[t] - remainder[:, t * TILE:(t + 1) * TILE]
        solved_out[t] = jnp.where(r == 0, leading, value) if t == 0 else value

    def leave(row, slot):
        return pltpu.make_async_copy(
            schur.at[pl.ds(0, height), columns(row)], updated_out.at[:, columns(row)], out_sem.at[slot])

    def finish(d, carry):
        row = row_at(pos + half + d)
        keep = 1.0 - ((layer + row) == 0).astype(f32)
        s_top, s_low = split(schur[low_rows, columns(row)] * keep)
        schur[pl.ds(0, height), columns(row)] = schur[pl.ds(0, height), columns(row)] - product(
            q_cat[...], jnp.concatenate([s_top, s_low, s_top], axis=0), ((1,), (0,)))
        leave(row, d).start()
        return carry

    lax.fori_loop(1, rows, finish, 0)

    fwd(last, 0).wait_recv()
    fwd_name(last).wait_recv()
    bwd(last, 1).wait_recv()
    opposite = row_at(pos + half)
    schur[:, columns(opposite)] = double(remote(opposite, 0), 0, tall)
    finish(0, 0)

    for s in range(half):
        for h in range(2):
            if s < last or h == 0:
                fwd(s, h).wait_send()
            if s < last or h == 1:
                bwd(s, h).wait_send()
        fwd_name(s).wait_send()
        if s < last:
            bwd_name(s).wait_send()
    for copy in waits:
        copy.wait_send()
    for k in far:
        share(k).wait_send()
        hand(k, (c + cols - 2 * k) % cols).wait_send()
    hand(0, c).wait_send()

    @pl.when(r == 0)
    def _():
        for copy in lead_to(lead_own, 0, right) + lead_to(lead_own, 1, left):
            copy.wait_send()

    @pl.when((pos >= 1) & (pos < half))
    def _():
        for copy in lead_to(lead_all, 0, right):
            copy.wait_send()

    @pl.when(pos >= half + 2)
    def _():
        for copy in lead_to(lead_all, 1, left):
            copy.wait_send()

    def leaving(d, carry):
        leave(row_at(pos + half + d), d).wait()
        return carry

    lax.fori_loop(0, rows, leaving, 0)


def assemble(rows, cols, coef, primal, dual, sizes, names, damping, sides):
    half = rows // 2
    dma = pltpu.SemaphoreType.DMA
    vmem = pl.BlockSpec(memory_space=pltpu.VMEM)
    anywhere = pl.BlockSpec(memory_space=pl.ANY)
    layers, lines, _ = coef.shape
    slots = names.shape[1]
    own_blocks, order, _ = primal.shape
    blocks = cols * own_blocks
    height = layers * TILE
    tall = height + TILE
    return pl.pallas_call(
        functools.partial(exchange, rows, cols),
        out_shape=[
            jax.ShapeDtypeStruct((height, rows * TILE), f32),
            jax.ShapeDtypeStruct((height, TILE), f32),
            jax.ShapeDtypeStruct(sides.shape, f32),
        ],
        in_specs=[anywhere] * 3 + [pl.BlockSpec(memory_space=pltpu.SMEM)] + [vmem] * 3,
        out_specs=[anywhere, vmem, vmem],
        scratch_shapes=[
            pltpu.VMEM((rows, lines, TILE), f32),
            pltpu.VMEM((rows,) + names.shape[1:], jnp.int32),
            pltpu.VMEM(coef.shape, f32),
            pltpu.VMEM((lines, TILE), f32),
            pltpu.VMEM(names.shape[1:], jnp.int32),
            pltpu.VMEM(damping.shape, f32),
            pltpu.VMEM(sides.shape[1:], f32),
            pltpu.VMEM(primal.shape, f32),
            pltpu.VMEM(dual.shape, f32),
            pltpu.VMEM((blocks, order, order), f32),
            pltpu.VMEM((slots, tall, order), bf16),
            pltpu.VMEM((slots, tall, order), bf16),
            pltpu.VMEM((slots, tall, TILE), bf16),
            pltpu.VMEM((slots, 2 * TILE, order), bf16),
            pltpu.VMEM((slots, 2 * TILE, order), bf16),
            pltpu.VMEM((slots, 2 * TILE, TILE), bf16),
            pltpu.VMEM((tall, order), bf16),
            pltpu.VMEM((tall, order), bf16),
            pltpu.VMEM((4, 2 * TILE, order), bf16),
            pltpu.VMEM((4, 2 * TILE, order), bf16),
            pltpu.VMEM((blocks, tall, order), bf16),
            pltpu.VMEM((blocks, tall, order), bf16),
            pltpu.VMEM((2 * tall, 2 * TILE), f32),
            pltpu.VMEM((tall, rows * TILE), f32),
            pltpu.VMEM((tall, TILE), f32),
            pltpu.VMEM((TILE, 2 * TILE), f32),
            pltpu.VMEM((height, 3 * TILE), bf16),
        ]
        + [dma((7,)), dma((rows,))] + [dma((half, 2))] * 4 + [dma((half,))] * 4 + [dma((2, 4)), dma((4,))]
        + [dma((cols,))] * 4 + [dma((cols, own_blocks))] * 4,
        compiler_params=pltpu.CompilerParams(collective_id=0, has_side_effects=True),
    )(coef, primal, dual, sizes, names, damping, sides)


def local(coefficients, support, primal, dual_inverse, block_sizes, damping, right_sides):
    col_index = lax.axis_index("cols")
    rows = lax.axis_size("rows")
    cols = lax.axis_size("cols")
    layers, tile, slots, order = coefficients.shape
    groups = order // TILE
    span = TILE * rows
    col_width = layers * span // cols
    coef = coefficients.reshape(layers, tile, slots, groups, TILE).transpose(0, 1, 3, 2, 4)
    coef = coef.reshape(layers, tile * slots * groups, TILE)
    names = jnp.transpose(support, (0, 2, 1))
    updated, panel, solved = assemble(rows, cols, coef, primal, dual_inverse, block_sizes, names, damping, right_sides)
    if span != col_width:
        updated = lax.dynamic_slice_in_dim(updated, (col_index * col_width) % span, col_width, 1)
    return updated.reshape(layers, tile, col_width), panel.reshape(layers, tile, TILE), solved


def solution(mesh):
    in_specs = (
        P(None, "rows", None, None),
        P(None, "rows", None),
        P("cols", None, None),
        P("cols", None, None),
        P("cols"),
        P(None, "rows"),
        P(None, "cols", "rows"),
    )
    out_specs = (P(None, "rows", "cols"), P(None, "rows", None), P(None, "cols", "rows"))
    return jax.shard_map(local, mesh=mesh, in_specs=in_specs, out_specs=out_specs, check_vma=False)
```
